768 devices in a mesh: region: 2 (over core), island: 12 (over z_hi, x), dev: 32 (over z_lo, y).
Axes of the slice: x: 4, y: 8, z: 12 (z_hi: 3, z_lo: 4; z = z_hi * 4 + z_lo), core: 2. Of those that a mesh axis runs over, the one named last changes fastest.
Arguments:
- activations: bfloat16 [196608, 2560], P(('region', 'island', 'dev')), may hold values from -6 to 6
- cotangent: bfloat16 [196608, 512], P(('region', 'island', 'dev')), may hold values from -6 to 6
- island_weight: float32 [2, 12, 2560, 512], P('region', 'island', 'dev'), may hold values from -6 to 6
- adam_first: float32 [2, 12, 2560, 512], P('region', 'island', 'dev'), may hold values from -6 to 6
- adam_second: float32 [2, 12, 2560, 512], P('region', 'island', 'dev'), may hold values from 0.01 to 1
- region_anchor: float32 [2, 2560, 512], P('region', 'dev'), may hold values from -6 to 6
- region_momentum: float32 [2, 2560, 512], P('region', 'dev'), may hold values from -6 to 6
- global_anchor: float32 [2560, 512], P('dev'), may hold values from -6 to 6
- global_momentum: float32 [2560, 512], P('dev'), may hold values from -6 to 6
Outputs:
- first_new: float32 [2, 12, 2560, 512], P('region', 'island', 'dev')
- second_new: float32 [2, 12, 2560, 512], P('region', 'island', 'dev')
- region_velocity: float32 [2, 2560, 512], P('region', 'dev')
- global_velocity: float32 [2560, 512], P('dev')
- global_new: float32 [2560, 512], P('dev')
- next_keys: bfloat16 [196608, 512], P(('region', 'island', 'dev'))
The draws below stay inside these ranges and needn't reach their ends.
All inputs are finite; a program needn't handle non-finite values.
Results may differ from the reference program's by a relative error of at most 0.0049.
Values may be sent and summed in bfloat16 or wider, within the bound.
A program may use at most 32 MiB of HBM per device.

```python
import math
import jax
import jax.numpy as jnp
from jax import lax

DW = 2560
KV = 512
TOK_DEV = 256
TOKENS = 196608
N_REGION = 2
N_ISLAND = 12
N_DEV = 32


def level_of(own_key, shape, split, smallest, top_value):
    def one(dim, blocks):
        heights = jax.random.uniform(jax.random.fold_in(jax.random.fold_in(own_key, 6), dim), (blocks,), jnp.float32, smallest / len(split), top_value / len(split))
        return jnp.repeat(jnp.exp(heights), shape[dim] // blocks).reshape((-1,) + (1,) * (len(shape) - dim - 1))

    loudness = one(*split[0])
    for cut in split[1:]:
        loudness = loudness * one(*cut)
    return loudness


def bell_draw(key, shape, deviation, most, shards=(), dtype=jnp.bfloat16):
    gain = level_of(key, shape, shards, -0.22, 0.18) if shards else 1.0
    array = jax.random.normal(key, shape, jnp.float32) * deviation * gain
    return jnp.minimum(jnp.maximum(array, -most), most).astype(dtype)


def setup_inputs(seed: int = 0) -> dict:
    key_list = jax.random.split(jax.random.key(seed), 10)
    activations = bell_draw(key_list[0], (TOKENS, DW), 1.0, 6.0, ((0, 768),))
    cotangent = bell_draw(key_list[1], (TOKENS, KV), 1.0, 6.0, ((0, 768),))
    island_weight = bell_draw(key_list[2], (N_REGION, N_ISLAND, DW, KV), 1.0, 6.0, ((0, 2), (1, 12), (2, 32)), jnp.float32)
    adam_first = bell_draw(key_list[3], (N_REGION, N_ISLAND, DW, KV), 1.0, 6.0, ((0, 2), (1, 12), (2, 32)), jnp.float32)
    adam_second = jnp.clip(jnp.exp(math.log(1.0) - 4.6051702 * jax.random.uniform(key_list[4], (N_REGION, N_ISLAND, DW, KV), jnp.float32) ** level_of(key_list[4], (N_REGION, N_ISLAND, DW, KV), ((0, 2), (1, 12), (2, 32)), -0.2, 0.2)), 0.01, 1.0)
    region_anchor = bell_draw(key_list[5], (N_REGION, DW, KV), 1.0, 6.0, ((0, 2), (1, 32)), jnp.float32)
    region_momentum = bell_draw(key_list[6], (N_REGION, DW, KV), 0.5, 6.0, ((0, 2), (1, 32)), jnp.float32)
    global_anchor = bell_draw(key_list[7], (DW, KV), 1.0, 6.0, ((0, 32),), jnp.float32)
    global_momentum = bell_draw(key_list[8], (DW, KV), 0.5, 6.0, ((0, 32),), jnp.float32)
    return {"activations": activations, "cotangent": cotangent, "island_weight": island_weight, "adam_first": adam_first, "adam_second": adam_second, "region_anchor": region_anchor, "region_momentum": region_momentum, "global_anchor": global_anchor, "global_momentum": global_momentum}


beta_first = 0.9
beta_second = 0.999
adam_eps = 1e-08
inner_rate = 0.05
weight_decay = 0.1
region_mu = 0.9
region_rate = 0.7
global_mu = 0.9
global_rate = 0.7

def island_gradient(pair):
    act_part, cot_part = pair
    partials = jnp.einsum('ntd,ntk->ndk', act_part.astype(jnp.float32), cot_part.astype(jnp.float32))
    rounded = lax.optimization_barrier(partials.astype(jnp.bfloat16)).astype(jnp.float32)
    return lax.optimization_barrier(jnp.sum(rounded, axis=0))

def reference(activations, cotangent, island_weight, adam_first, adam_second, region_anchor, region_momentum, global_anchor, global_momentum):
    groups = N_REGION * N_ISLAND
    act_blocks = activations.reshape(groups, N_DEV, TOK_DEV, DW)
    cot_blocks = cotangent.reshape(groups, N_DEV, TOK_DEV, KV)
    summed = lax.map(island_gradient, (act_blocks, cot_blocks)).reshape(N_REGION, N_ISLAND, DW, KV)
    gradient = summed * (1.0 / math.sqrt(TOK_DEV * N_DEV))
    first_new = beta_first * adam_first + (1.0 - beta_first) * gradient
    second_new = beta_second * adam_second + (1.0 - beta_second) * gradient * gradient
    inner = island_weight - inner_rate * (first_new / (jnp.sqrt(second_new) + adam_eps) + weight_decay * island_weight)
    island_delta = region_anchor[:, None] - inner
    region_mean = lax.optimization_barrier(jnp.sum(island_delta, axis=1)) / N_ISLAND
    region_velocity = region_mu * region_momentum + region_mean
    region_params = region_anchor - region_rate * (region_mean + region_mu * region_velocity)
    global_mean = lax.optimization_barrier(jnp.sum(global_anchor[None] - region_params, axis=0)) / N_REGION
    global_velocity = global_mu * global_momentum + global_mean
    global_new = global_anchor - global_rate * (global_mean + global_mu * global_velocity)
    projected = jnp.dot(activations, global_new.astype(jnp.bfloat16), preferred_element_type=jnp.float32)
    next_keys = (projected * (1.0 / math.sqrt(DW))).astype(jnp.bfloat16)
    return (first_new, second_new, region_velocity, global_velocity, global_new, next_keys)
```

```python
import functools
import math

import jax
import jax.numpy as jnp
from jax import lax
from jax.experimental import pallas as pl
from jax.experimental.pallas import tpu as pltpu
from jax.sharding import Mesh
from jax.sharding import PartitionSpec as P

DW = 2560
KV = 512
TOK = 256
ROWS = 80
LB = 128
N_Y = 8
N_ZL = 4
N_ZH = 3
N_X = 4
MESH = pl.DeviceIdType.MESH
BF = jnp.bfloat16
F32 = jnp.float32

beta_first = 0.9
beta_second = 0.999
adam_eps = 1e-08
inner_rate = 0.05
weight_decay = 0.1
region_mu = 0.9
region_rate = 0.7
global_mu = 0.9
global_rate = 0.7

W_, M_, V_, RA, RM, GA, GM = range(7)
O_FIRST, O_SECOND, O_RV, O_GV, O_GN = range(5)
SIGN = (1, -1)


def hops(d, lb):
    return 4 if (lb % 2 == 0) == (d == 0) else 3


def kernel(
    act_hbm, cot_hbm, w_hbm, m_hbm, v_hbm, ra_hbm, rm_hbm, ga_hbm, gm_hbm,
    of_hbm, os_hbm, orv_hbm, ogv_hbm, ogn_hbm, okeys_hbm,
    act, cot, state, part, yrec, ysum, zrec, zfar, ypart, yfar, delta, xrec, trec,
    gap, means, wfull, ksend, krec, outs, keys,
    in_sem, out_sem, act_sem, ys_sem, yr_sem, zs_sem, zr_sem, fs_sem, fr_sem,
    xs_sem, xr_sem, ts_sem, tr_sem, g_sem, ms_sem, mr_sem, wxs_sem, wxr_sem,
    wzs_sem, wzr_sem, wys_sem, wyr_sem, k_sem,
):
    r = lax.axis_index("region")
    zh = lax.axis_index("zh")
    x = lax.axis_index("x")
    zl = lax.axis_index("zl")
    y = lax.axis_index("y")
    z = zh * 4 + zl
    other = {"region": 1 - r}

    def to_z(off):
        t = lax.rem(z + off + 12, 12)
        return {"zh": t // 4, "zl": lax.rem(t, 4)}

    def to_y(off):
        return {"y": lax.rem(y + off + N_Y, N_Y)}

    def to_x(off):
        return {"x": lax.rem(x + off + N_X, N_X)}

    def remote(src, dst, ssem, rsem, dev):
        return pltpu.make_async_remote_copy(
            src_ref=src, dst_ref=dst, send_sem=ssem, recv_sem=rsem,
            device_id=dev, device_id_type=MESH,
        )

    drains = []

    def go(c):
        c.start()
        drains.append(c.wait_send)

    def go_if(cond, make):
        @pl.when(cond)
        def _():
            make().start()

        def drain():
            @pl.when(cond)
            def _():
                make().wait_send()

        drains.append(drain)

    loads = [
        pltpu.make_async_copy(act_hbm, act.at[0], in_sem.at[0]),
        pltpu.make_async_copy(cot_hbm, cot, in_sem.at[1]),
    ]
    for i, ref in enumerate((w_hbm, m_hbm, v_hbm, ra_hbm, rm_hbm, ga_hbm, gm_hbm)):
        loads.append(pltpu.make_async_copy(ref, state.at[i], in_sem.at[2 + i]))
    for c in loads:
        c.start()
    stores = [
        pltpu.make_async_copy(outs.at[i], o, out_sem.at[i])
        for i, o in enumerate((of_hbm, os_hbm, orv_hbm, ogv_hbm, ogn_hbm))
    ]

    barrier = pltpu.get_barrier_semaphore()
    peers = [other] + [to_y(k) for k in (1, -1)] + [to_x(k) for k in (1, 2, 3)]
    peers += [to_z(k) for k in (-4, -3, -2, -1, 1, 2, 3, 4)]
    for dev in peers:
        pl.semaphore_signal(barrier, inc=1, device_id=dev, device_id_type=MESH)

    loads[0].wait()
    loads[1].wait()

    def ysend(d, lb, s):
        t = lax.rem(y + SIGN[d] * (hops(d, lb) - s) + N_Y, N_Y)
        if lb == 3:
            src = ypart.at[t] if s == 0 else yfar.at[d, s - 1]
            dst = yfar.at[d, s]
        else:
            src = part.at[lb, t] if s == 0 else yrec.at[d, lb, s - 1]
            dst = yrec.at[d, lb, s]
        return remote(
            src, dst, ys_sem.at[d, lb, s], yr_sem.at[d, lb, s], to_y(SIGN[d])
        )

    def ystart(lb):
        for d in range(2):
            go(ysend(d, lb, 0))

    def ystep(lb, s):
        for d in range(2):
            n = hops(d, lb)
            if s >= n:
                continue
            ysend(d, lb, s).wait_recv()
            if s < n - 1:
                t = lax.rem(y + SIGN[d] * (n - s - 1) + N_Y, N_Y)
                if lb == 3:
                    yfar[d, s] = (
                        yfar[d, s].astype(F32) + ypart[t].astype(F32)
                    ).astype(BF)
                else:
                    yrec[d, lb, s] = (
                        yrec[d, lb, s].astype(F32) + part[lb, t].astype(F32)
                    ).astype(BF)
                go(ysend(d, lb, s + 1))

    def zsend(lb, k):
        t = lax.rem(zl + k, N_ZL)
        return remote(
            ysum.at[lb, t], zrec.at[lb, zl], zs_sem.at[lb, k - 1],
            zr_sem.at[lb, k - 1], {"zl": t},
        )

    def zrecv(lb, k):
        src = lax.rem(zl + N_ZL - k, N_ZL)
        return remote(
            ysum.at[lb, zl], zrec.at[lb, src], zs_sem.at[lb, k - 1],
            zr_sem.at[lb, k - 1], {"zl": src},
        )

    def yfinal(lb):
        total = (
            part[lb, y].astype(F32)
            + yrec[0, lb, hops(0, lb) - 1].astype(F32)
            + yrec[1, lb, hops(1, lb) - 1].astype(F32)
        )
        ysum[lb] = total.astype(BF)
        for k in (1, 2, 3):
            go(zsend(lb, k))

    def fsend(k):
        t = lax.rem(zl + k, N_ZL)
        return remote(
            part.at[3, :, t], zfar.at[k - 1], fs_sem.at[k - 1], fr_sem.at[k - 1],
            {"zl": t},
        )

    def far():
        for k in (1, 2, 3):
            fsend(k).wait_recv()
        for t in range(N_Y):
            total = part[3, t, zl].astype(F32)
            for k in range(3):
                total = total + zfar[k, t].astype(F32)
            ypart[t] = total.astype(BF)
        ystart(3)

    def xsend(lb):
        return remote(
            delta.at[lb], xrec.at[x], xs_sem.at[lb], xr_sem.at[x], {"x": lb}
        )

    def adam(lb):
        if lb == 3:
            g = (
                ypart[y].astype(F32)
                + yfar[0, hops(0, 3) - 1].astype(F32)
                + yfar[1, hops(1, 3) - 1].astype(F32)
            )
        else:
            for k in (1, 2, 3):
                zrecv(lb, k).wait_recv()
            g = ysum[lb, zl].astype(F32)
            for k in (1, 2, 3):
                g = g + zrec[lb, lax.rem(zl + k, N_ZL)].astype(F32)
        lanes = slice(lb * LB, (lb + 1) * LB)
        gradient = g * (1.0 / math.sqrt(TOK * 32))
        first = beta_first * state[M_, :, lanes] + (1.0 - beta_first) * gradient
        second = (
            beta_second * state[V_, :, lanes]
            + (1.0 - beta_second) * gradient * gradient
        )
        weight = state[W_, :, lanes]
        inner = weight - inner_rate * (
            first / (jnp.sqrt(second) + adam_eps) + weight_decay * weight
        )
        outs[O_FIRST, :, lanes] = first
        outs[O_SECOND, :, lanes] = second
        delta[lb] = (state[RA, :, lanes] - inner).astype(BF)
        go_if(x != lb, lambda: xsend(lb))

    mine = pl.ds(pl.multiple_of(x * LB, LB), LB)

    def tsend(k):
        return remote(
            trec.at[zh], trec.at[zh], ts_sem.at[k - 1], tr_sem.at[k - 1],
            {"zh": lax.rem(zh + k, N_ZH)},
        )

    def trecv(k):
        src = lax.rem(zh + N_ZH - k, N_ZH)
        return remote(
            trec.at[zh], trec.at[src], ts_sem.at[k - 1], tr_sem.at[k - 1], {"zh": src}
        )

    def gsend():
        return remote(gap.at[r], gap.at[r], g_sem.at[0], g_sem.at[1], other)

    def owner_a(h):
        @pl.when(x // 2 == h)
        def _():
            t = delta[x].astype(F32)
            for k in (1, 2, 3):
                src = lax.rem(x + k, N_X)
                remote(
                    delta.at[0], xrec.at[src], xs_sem.at[0], xr_sem.at[src], {"x": src}
                ).wait_recv()
                t = t + xrec[src].astype(F32)
            trec[zh] = t
            for k in (1, 2):
                tsend(k).start()

    def owner_b(h):
        @pl.when(x // 2 == h)
        def _():
            for k in (1, 2):
                trecv(k).wait_recv()
            region_mean = ((trec[0] + trec[1]) + trec[2]) / 12
            region_velocity = region_mu * state[RM, :, mine] + region_mean
            region_params = state[RA, :, mine] - region_rate * (
                region_mean + region_mu * region_velocity
            )
            gap[r] = state[GA, :, mine] - region_params
            gsend().start()
            means[x, 0] = region_mean

    def wxsend(h, k):
        slot = wfull.at[h, zl, y]
        return remote(slot, slot, wxs_sem.at[k - 1], wxr_sem.at[h], to_x(k))

    def msend(k):
        return remote(
            means.at[x], means.at[x], ms_sem.at[k - 1], mr_sem.at[x], to_x(k)
        )

    def owner_c(h):
        @pl.when(x // 2 == h)
        def _():
            remote(
                gap.at[r], gap.at[1 - r], g_sem.at[0], g_sem.at[1], other
            ).wait_recv()
            global_mean = (gap[0] + gap[1]) / 2
            global_velocity = global_mu * state[GM, :, mine] + global_mean
            global_new = state[GA, :, mine] - global_rate * (
                global_mean + global_mu * global_velocity
            )

            @pl.when(lax.rem(x, 2) == r)
            def _():
                wfull[h, zl, y] = global_new.astype(BF)
                for k in (1, 2, 3):
                    wxsend(h, k).start()

            means[x, 1] = global_mean
            for k in (1, 2, 3):
                msend(k).start()

    def wz_offs(h):
        return (1, -1, 2 if h == 0 else -2)

    def wzsend(h, i):
        slot = wfull.at[h, zl, y]
        return remote(
            slot, slot, wzs_sem.at[h, i], wzr_sem.at[h, i], to_z(wz_offs(h)[i])
        )

    def wzrecv(h, i):
        slot = wfull.at[h, lax.rem(zl - wz_offs(h)[i] + 4, 4), y]
        return remote(
            slot, slot, wzs_sem.at[h, i], wzr_sem.at[h, i], to_z(-wz_offs(h)[i])
        )

    def wz(h):
        @pl.when(x != 2 * h + r)
        def _():
            slot = wfull.at[h, zl, y]
            remote(
                slot, slot, wxs_sem.at[0], wxr_sem.at[h], {"x": 2 * h + r}
            ).wait_recv()

        for i in range(3):
            go(wzsend(h, i))

    def wysend(d, h, s):
        slot = wfull.at[h, :, lax.rem(y - SIGN[d] * s + N_Y, N_Y)]
        return remote(
            slot, slot, wys_sem.at[d, h, s], wyr_sem.at[d, h, s], to_y(SIGN[d])
        )

    def wyrecv(d, h, s):
        slot = wfull.at[h, :, lax.rem(y - SIGN[d] * (s + 1) + N_Y, N_Y)]
        return remote(
            slot, slot, wys_sem.at[d, h, s], wyr_sem.at[d, h, s], to_y(-SIGN[d])
        )

    def wystart(h):
        for i in range(3):
            wzrecv(h, i).wait_recv()
        for d in range(2):
            go(wysend(d, h, 0))

    def wystep(h, s):
        for d in range(2):
            n = hops(d, h)
            if s >= n:
                continue
            wyrecv(d, h, s).wait_recv()
            if s + 1 < n:
                go(wysend(d, h, s + 1))

    def replicated():
        for lb in range(4):
            @pl.when(x != lb)
            def _():
                remote(
                    means.at[x], means.at[lb], ms_sem.at[0], mr_sem.at[lb], {"x": lb}
                ).wait_recv()

            lanes = slice(lb * LB, (lb + 1) * LB)
            rmean = means[lb, 0]
            gmean = means[lb, 1]
            outs[O_RV, :, lanes] = region_mu * state[RM, :, lanes] + rmean
            gvel = global_mu * state[GM, :, lanes] + gmean
            outs[O_GV, :, lanes] = gvel
            outs[O_GN, :, lanes] = state[GA, :, lanes] - global_rate * (
                gmean + global_mu * gvel
            )
        for i in (O_RV, O_GV, O_GN):
            stores[i].start()
            drains.append(stores[i].wait)

    scale = 1.0 / math.sqrt(DW)

    def kcopy(h):
        return remote(ksend.at[h], krec.at[h], k_sem.at[h], k_sem.at[2 + h], other)

    def project(h):
        rhs = wfull[h].reshape(DW, LB)
        ksend[h] = (
            jnp.dot(act[1], rhs, preferred_element_type=F32) * scale
        ).astype(BF)
        go(kcopy(h))
        keys[:, pl.ds(pl.multiple_of((2 * h + r) * LB, LB), LB)] = (
            jnp.dot(act[0], rhs, preferred_element_type=F32) * scale
        ).astype(BF)

    act_copy = remote(act.at[0], act.at[1], act_sem.at[0], act_sem.at[1], other)
    for h in (1, 0):
        rhs = cot[:, h * 256 : (h + 1) * 256]
        for q in range(N_ZL):
            lhs = act[0, :, q * 640 : (q + 1) * 640]
            term = lax.dot_general(
                lhs, rhs, (((0,), (0,)), ((), ())), preferred_element_type=F32
            ).astype(BF)
            for b in range(2):
                for t in range(N_Y):
                    part[2 * h + b, t, q] = term[
                        t * ROWS : (t + 1) * ROWS, b * LB : (b + 1) * LB
                    ]
        if h == 1:
            pl.semaphore_wait(barrier, len(peers))
            for k in (1, 2, 3):
                go(fsend(k))
            ystart(2)
        else:
            ystart(0)
            ystart(1)
    go(act_copy)
    for s in range(2):
        for lb in (2, 0, 1):
            ystep(lb, s)
    far()
    for lb in (2, 0, 1):
        ystep(lb, 2)
    ystep(3, 0)
    for lb in (2, 0, 1):
        ystep(lb, 3)
        yfinal(lb)
    for s in (1, 2, 3):
        ystep(3, s)
    for c in loads[2:]:
        c.wait()
    for lb in (3, 2, 0, 1):
        adam(lb)
    for i in (O_FIRST, O_SECOND):
        stores[i].start()
        drains.append(stores[i].wait)
    for stage in (owner_a, owner_b, owner_c, wz, wystart):
        for h in range(2):
            stage(h)
    for s in range(4):
        for h in range(2):
            wystep(h, s)
        if s == 1:
            replicated()
    act_copy.wait_recv()
    project(0)
    project(1)
    for h in range(2):
        kcopy(h).wait_recv()
        keys[:, pl.ds(pl.multiple_of((2 * h + 1 - r) * LB, LB), LB)] = krec[h]
    k_store = pltpu.make_async_copy(keys, okeys_hbm, out_sem.at[5])
    k_store.start()
    for drain in drains:
        drain()
    for k in (1, 2):
        tsend(k).wait_send()
    gsend().wait_send()
    for k in (1, 2, 3):
        msend(k).wait_send()

    @pl.when(lax.rem(x, 2) == r)
    def _():
        for k in (1, 2, 3):
            wxsend(0, k).wait_send()

    k_store.wait()


def hand_over(*refs):
    copies = [
        pltpu.make_async_copy(refs[i], refs[6 + i], refs[12].at[i]) for i in range(6)
    ]
    for c in copies:
        c.start()
    for c in copies:
        c.wait()


def body(act, cot, w, m, v, ra, rm, ga, gm):
    dma = pltpu.SemaphoreType.DMA
    flat = lambda a: a.reshape(ROWS, KV)
    out = pl.pallas_call(
        kernel,
        out_shape=[jax.ShapeDtypeStruct((ROWS, KV), F32)] * 5
        + [jax.ShapeDtypeStruct((TOK, KV), BF)],
        in_specs=[pl.BlockSpec(memory_space=pl.ANY)] * 9,
        out_specs=[pl.BlockSpec(memory_space=pl.ANY)] * 6,
        scratch_shapes=[
            pltpu.VMEM((2, TOK, DW), BF),
            pltpu.VMEM((TOK, KV), BF),
            pltpu.VMEM((7, ROWS, KV), F32),
            pltpu.VMEM((4, N_Y, N_ZL, ROWS, LB), BF),
            pltpu.VMEM((2, 3, 4, N_ZL, ROWS, LB), BF),
            pltpu.VMEM((3, N_ZL, ROWS, LB), BF),
            pltpu.VMEM((3, N_ZL, ROWS, LB), BF),
            pltpu.VMEM((3, N_Y, ROWS, LB), BF),
            pltpu.VMEM((N_Y, ROWS, LB), BF),
            pltpu.VMEM((2, 4, ROWS, LB), BF),
            pltpu.VMEM((4, ROWS, LB), BF),
            pltpu.VMEM((N_X, ROWS, LB), BF),
            pltpu.VMEM((N_ZH, ROWS, LB), F32),
            pltpu.VMEM((2, ROWS, LB), F32),
            pltpu.VMEM((N_X, 2, ROWS, LB), F32),
            pltpu.VMEM((2, N_ZL, N_Y, ROWS, LB), BF),
            pltpu.VMEM((2, TOK, LB), BF),
            pltpu.VMEM((2, TOK, LB), BF),
            pltpu.VMEM((5, ROWS, KV), F32),
            pltpu.VMEM((TOK, KV), BF),
            dma((9,)),
            dma((6,)),
            dma((2,)),
            dma((2, 4, 4)),
            dma((2, 4, 4)),
            dma((3, 3)),
            dma((3, 3)),
            dma((3,)),
            dma((3,)),
            dma((4,)),
            dma((4,)),
            dma((2,)),
            dma((2,)),
            dma((2,)),
            dma((3,)),
            dma((4,)),
            dma((3,)),
            dma((2,)),
            dma((2, 3)),
            dma((2, 3)),
            dma((2, 2, 4)),
            dma((2, 2, 4)),
            dma((4,)),
        ],
        compiler_params=pltpu.CompilerParams(
            collective_id=0, has_side_effects=True, vmem_limit_bytes=60 * 1024 * 1024
        ),
        name="outer_sync",
    )(act, cot, *map(flat, (w, m, v, ra, rm, ga, gm)))
    first, second, rv, gv, gn, keys = pl.pallas_call(
        hand_over,
        out_shape=[jax.ShapeDtypeStruct(o.shape, o.dtype) for o in out],
        in_specs=[pl.BlockSpec(memory_space=pltpu.VMEM)] * 6,
        out_specs=[pl.BlockSpec(memory_space=pl.ANY)] * 6,
        scratch_shapes=[dma((6,))],
        name="hand_over",
    )(*out)
    return (
        first.reshape(1, 1, ROWS, KV),
        second.reshape(1, 1, ROWS, KV),
        rv.reshape(1, ROWS, KV),
        gv,
        gn,
        keys,
    )


def solution(mesh):
    finer = Mesh(
        mesh.devices.reshape(2, N_ZH, N_X, N_ZL, N_Y), ("region", "zh", "x", "zl", "y")
    )
    island = ("zh", "x")
    dev = ("zl", "y")
    every = ("region", "zh", "x", "zl", "y")
    return jax.shard_map(
        body,
        mesh=finer,
        in_specs=(
            P(every, None),
            P(every, None),
            P("region", island, dev, None),
            P("region", island, dev, None),
            P("region", island, dev, None),
            P("region", dev, None),
            P("region", dev, None),
            P(dev, None),
            P(dev, None),
        ),
        out_specs=(
            P("region", island, dev, None),
            P("region", island, dev, None),
            P("region", dev, None),
            P(dev, None),
            P(dev, None),
            P(every, None),
        ),
        check_vma=False,
    )
```

```python
import functools
import math

import jax
import jax.numpy as jnp
from jax import lax
from jax.experimental import pallas as pl
from jax.experimental.pallas import tpu as pltpu
from jax.sharding import Mesh
from jax.sharding import PartitionSpec as P

DW = 2560
KV = 512
TOK = 256
ROWS = 80
LB = 128
N_Y = 8
N_ZL = 4
N_ZH = 3
N_X = 4
MESH = pl.DeviceIdType.MESH
BF = jnp.bfloat16
F32 = jnp.float32

beta_first = 0.9
beta_second = 0.999
adam_eps = 1e-08
inner_rate = 0.05
weight_decay = 0.1
region_mu = 0.9
region_rate = 0.7
global_mu = 0.9
global_rate = 0.7

W_, M_, V_, RA, RM, GA, GM = range(7)
O_FIRST, O_SECOND, O_RV, O_GV, O_GN = range(5)
SIGN = (1, -1)


def hops(d, lb):
    return 4 if (lb % 2 == 0) == (d == 0) else 3


def kernel(
    act_hbm, cot_hbm, w_hbm, m_hbm, v_hbm, ra_hbm, rm_hbm, ga_hbm, gm_hbm,
    of_hbm, os_hbm, orv_hbm, ogv_hbm, ogn_hbm, okeys_hbm,
    act, cot, state, part, yrec, ysum, zrec, zfar, ypart, yfar, delta, xrec, trec,
    gap, means, wfull, ksend, krec, outs, keys,
    in_sem, out_sem, act_sem, ys_sem, yr_sem, zs_sem, zr_sem, fs_sem, fr_sem,
    xs_sem, xr_sem, ts_sem, tr_sem, g_sem, ms_sem, mr_sem, wxs_sem, wxr_sem,
    wz0s_sem, wz0r_sem, wy0s_sem, wy0r_sem, wy1s_sem, wy1r_sem, wz1s_sem, wz1r_sem,
    k_sem,
):
    r = lax.axis_index("region")
    zh = lax.axis_index("zh")
    x = lax.axis_index("x")
    zl = lax.axis_index("zl")
    y = lax.axis_index("y")
    z = zh * 4 + zl
    other = {"region": 1 - r}

    def to_z(off):
        t = lax.rem(z + off + 12, 12)
        return {"zh": t // 4, "zl": lax.rem(t, 4)}

    def to_y(off):
        return {"y": lax.rem(y + off + N_Y, N_Y)}

    def to_x(off):
        return {"x": lax.rem(x + off + N_X, N_X)}

    def remote(src, dst, ssem, rsem, dev):
        return pltpu.make_async_remote_copy(
            src_ref=src, dst_ref=dst, send_sem=ssem, recv_sem=rsem,
            device_id=dev, device_id_type=MESH,
        )

    drains = []

    def go(c):
        c.start()
        drains.append(c.wait_send)

    def go_if(cond, make):
        @pl.when(cond)
        def _():
            make().start()

        def drain():
            @pl.when(cond)
            def _():
                make().wait_send()

        drains.append(drain)

    loads = [
        pltpu.make_async_copy(act_hbm, act.at[0], in_sem.at[0]),
        pltpu.make_async_copy(cot_hbm, cot, in_sem.at[1]),
    ]
    for i, ref in enumerate((w_hbm, m_hbm, v_hbm, ra_hbm, rm_hbm, ga_hbm, gm_hbm)):
        loads.append(pltpu.make_async_copy(ref, state.at[i], in_sem.at[2 + i]))
    for c in loads:
        c.start()
    stores = [
        pltpu.make_async_copy(outs.at[i], o, out_sem.at[i])
        for i, o in enumerate((of_hbm, os_hbm, orv_hbm, ogv_hbm, ogn_hbm))
    ]

    barrier = pltpu.get_barrier_semaphore()
    peers = [other] + [to_y(k) for k in (1, -1)] + [to_x(k) for k in (1, 2, 3)]
    peers += [to_z(k) for k in (-4, -3, -2, -1, 1, 2, 3, 4)]
    for dev in peers:
        pl.semaphore_signal(barrier, inc=1, device_id=dev, device_id_type=MESH)

    loads[0].wait()
    loads[1].wait()

    def ysend(d, lb, s):
        t = lax.rem(y + SIGN[d] * (hops(d, lb) - s) + N_Y, N_Y)
        if lb == 3:
            src = ypart.at[t] if s == 0 else yfar.at[d, s - 1]
            dst = yfar.at[d, s]
        else:
            src = part.at[lb, t] if s == 0 else yrec.at[d, lb, s - 1]
            dst = yrec.at[d, lb, s]
        return remote(
            src, dst, ys_sem.at[d, lb, s], yr_sem.at[d, lb, s], to_y(SIGN[d])
        )

    def ystart(lb):
        for d in range(2):
            go(ysend(d, lb, 0))

    def ystep(lb, s):
        for d in range(2):
            n = hops(d, lb)
            if s >= n:
                continue
            ysend(d, lb, s).wait_recv()
            if s < n - 1:
                t = lax.rem(y + SIGN[d] * (n - s - 1) + N_Y, N_Y)
                if lb == 3:
                    yfar[d, s] = (
                        yfar[d, s].astype(F32) + ypart[t].astype(F32)
                    ).astype(BF)
                else:
                    yrec[d, lb, s] = (
                        yrec[d, lb, s].astype(F32) + part[lb, t].astype(F32)
                    ).astype(BF)
                go(ysend(d, lb, s + 1))

    def zsend(lb, k):
        t = lax.rem(zl + k, N_ZL)
        return remote(
            ysum.at[lb, t], zrec.at[lb, zl], zs_sem.at[lb, k - 1],
            zr_sem.at[lb, k - 1], {"zl": t},
        )

    def zrecv(lb, k):
        src = lax.rem(zl + N_ZL - k, N_ZL)
        return remote(
            ysum.at[lb, zl], zrec.at[lb, src], zs_sem.at[lb, k - 1],
            zr_sem.at[lb, k - 1], {"zl": src},
        )

    def yfinal(lb):
        total = (
            part[lb, y].astype(F32)
            + yrec[0, lb, hops(0, lb) - 1].astype(F32)
            + yrec[1, lb, hops(1, lb) - 1].astype(F32)
        )
        ysum[lb] = total.astype(BF)
        for k in (1, 2, 3):
            go(zsend(lb, k))

    def fsend(k):
        t = lax.rem(zl + k, N_ZL)
        return remote(
            part.at[3, :, t], zfar.at[k - 1], fs_sem.at[k - 1], fr_sem.at[k - 1],
            {"zl": t},
        )

    def far():
        for k in (1, 2, 3):
            fsend(k).wait_recv()
        for t in range(N_Y):
            total = part[3, t, zl].astype(F32)
            for k in range(3):
                total = total + zfar[k, t].astype(F32)
            ypart[t] = total.astype(BF)
        ystart(3)

    def xsend(lb):
        return remote(
            delta.at[lb], xrec.at[x], xs_sem.at[lb], xr_sem.at[x], {"x": lb}
        )

    def adam(lb):
        if lb == 3:
            g = (
                ypart[y].astype(F32)
                + yfar[0, hops(0, 3) - 1].astype(F32)
                + yfar[1, hops(1, 3) - 1].astype(F32)
            )
        else:
            for k in (1, 2, 3):
                zrecv(lb, k).wait_recv()
            g = ysum[lb, zl].astype(F32)
            for k in (1, 2, 3):
                g = g + zrec[lb, lax.rem(zl + k, N_ZL)].astype(F32)
        lanes = slice(lb * LB, (lb + 1) * LB)
        gradient = g * (1.0 / math.sqrt(TOK * 32))
        first = beta_first * state[M_, :, lanes] + (1.0 - beta_first) * gradient
        second = (
            beta_second * state[V_, :, lanes]
            + (1.0 - beta_second) * gradient * gradient
        )
        weight = state[W_, :, lanes]
        inner = weight - inner_rate * (
            first / (jnp.sqrt(second) + adam_eps) + weight_decay * weight
        )
        outs[O_FIRST, :, lanes] = first
        outs[O_SECOND, :, lanes] = second
        delta[lb] = (state[RA, :, lanes] - inner).astype(BF)
        go_if(x != lb, lambda: xsend(lb))

    mine = pl.ds(pl.multiple_of(x * LB, LB), LB)

    def tsend(k):
        return remote(
            trec.at[zh], trec.at[zh], ts_sem.at[k - 1], tr_sem.at[k - 1],
            {"zh": lax.rem(zh + k, N_ZH)},
        )

    def trecv(k):
        src = lax.rem(zh + N_ZH - k, N_ZH)
        return remote(
            trec.at[zh], trec.at[src], ts_sem.at[k - 1], tr_sem.at[k - 1], {"zh": src}
        )

    def gsend():
        return remote(gap.at[r], gap.at[r], g_sem.at[0], g_sem.at[1], other)

    def owner_a(h):
        @pl.when(x // 2 == h)
        def _():
            t = delta[x].astype(F32)
            for k in (1, 2, 3):
                src = lax.rem(x + k, N_X)
                remote(
                    delta.at[0], xrec.at[src], xs_sem.at[0], xr_sem.at[src], {"x": src}
                ).wait_recv()
                t = t + xrec[src].astype(F32)
            trec[zh] = t
            for k in (1, 2):
                tsend(k).start()

    def owner_b(h):
        @pl.when(x // 2 == h)
        def _():
            for k in (1, 2):
                trecv(k).wait_recv()
            region_mean = ((trec[0] + trec[1]) + trec[2]) / 12
            region_velocity = region_mu * state[RM, :, mine] + region_mean
            region_params = state[RA, :, mine] - region_rate * (
                region_mean + region_mu * region_velocity
            )
            gap[r] = state[GA, :, mine] - region_params
            gsend().start()
            means[x, 0] = region_mean

    def wxsend(h, k):
        slot = wfull.at[h, zl, y]
        return remote(slot, slot, wxs_sem.at[k - 1], wxr_sem.at[h], to_x(k))

    def msend(k):
        return remote(
            means.at[x], means.at[x], ms_sem.at[k - 1], mr_sem.at[x], to_x(k)
        )

    def owner_c(h):
        @pl.when(x // 2 == h)
        def _():
            remote(
                gap.at[r], gap.at[1 - r], g_sem.at[0], g_sem.at[1], other
            ).wait_recv()
            global_mean = (gap[0] + gap[1]) / 2
            global_velocity = global_mu * state[GM, :, mine] + global_mean
            global_new = state[GA, :, mine] - global_rate * (
                global_mean + global_mu * global_velocity
            )

            @pl.when(lax.rem(x, 2) == r)
            def _():
                wfull[h, zl, y] = global_new.astype(BF)
                for k in (1, 2, 3):
                    wxsend(h, k).start()

            means[x, 1] = global_mean
            for k in (1, 2, 3):
                msend(k).start()

    def wx(h):
        @pl.when(x != 2 * h + r)
        def _():
            slot = wfull.at[h, zl, y]
            remote(
                slot, slot, wxs_sem.at[0], wxr_sem.at[h], {"x": 2 * h + r}
            ).wait_recv()

    def near(off):
        return lax.rem(zl - off + N_ZL, N_ZL)

    def origin(d, s):
        return lax.rem(y - SIGN[d] * s + N_Y, N_Y)

    offs = (0, 1, -1, 2)

    def z0(j, off):
        slot = wfull.at[0, near(off), y]
        return slot, wz0s_sem.at[j - 1], wz0r_sem.at[j - 1]

    def z0send(j):
        slot, ssem, rsem = z0(j, 0)
        return remote(slot, slot, ssem, rsem, to_z(offs[j]))

    def z0recv(j):
        slot, ssem, rsem = z0(j, offs[j])
        return remote(slot, slot, ssem, rsem, to_z(-offs[j]))

    def y0send(d, j, s):
        slot = wfull.at[0, near(offs[j]), origin(d, s)]
        return remote(
            slot, slot, wy0s_sem.at[d, j, s], wy0r_sem.at[d, j, s], to_y(SIGN[d])
        )

    def y0recv(d, j, s):
        slot = wfull.at[0, near(offs[j]), origin(d, s + 1)]
        return remote(
            slot, slot, wy0s_sem.at[d, j, s], wy0r_sem.at[d, j, s], to_y(-SIGN[d])
        )

    def y0start(j):
        if j > 0:
            z0recv(j).wait_recv()
        for d in range(2):
            go(y0send(d, j, 0))

    def y0step(j, s):
        for d in range(2):
            if s < hops(d, j):
                y0recv(d, j, s).wait_recv()
                if s + 1 < hops(d, j):
                    go(y0send(d, j, s + 1))

    def y1(d, s, at):
        slot = wfull.at[1, zl, origin(d, at)]
        return slot, slot, wy1s_sem.at[d, s], wy1r_sem.at[d, s]

    def z1off(c, i):
        return (1, -1, 2 if c % 2 == 0 else -2)[i]

    def z1send(c, at, i):
        slot = wfull.at[1, zl, at]
        return remote(
            slot, slot, wz1s_sem.at[c, i], wz1r_sem.at[c, i], to_z(z1off(c, i))
        )

    def z1recv(c, at, i):
        slot = wfull.at[1, near(z1off(c, i)), at]
        return remote(
            slot, slot, wz1s_sem.at[c, i], wz1r_sem.at[c, i], to_z(-z1off(c, i))
        )

    pieces = [(0, y)]

    def y1start():
        for d in range(2):
            go(remote(*y1(d, 0, 0), to_y(SIGN[d])))
        for i in range(3):
            go(z1send(0, y, i))

    def y1step(s):
        for d in range(2):
            n = hops(d, 0)
            if s < n:
                remote(*y1(d, s, s + 1), to_y(-SIGN[d])).wait_recv()
                if s + 1 < n:
                    go(remote(*y1(d, s + 1, s + 1), to_y(SIGN[d])))
                c, at = len(pieces), origin(d, s + 1)
                pieces.append((c, at))
                for i in (2, 0, 1):
                    go(z1send(c, at, i))

    def replicated():
        for lb in range(4):
            @pl.when(x != lb)
            def _():
                remote(
                    means.at[x], means.at[lb], ms_sem.at[0], mr_sem.at[lb], {"x": lb}
                ).wait_recv()

            lanes = slice(lb * LB, (lb + 1) * LB)
            rmean = means[lb, 0]
            gmean = means[lb, 1]
            outs[O_RV, :, lanes] = region_mu * state[RM, :, lanes] + rmean
            gvel = global_mu * state[GM, :, lanes] + gmean
            outs[O_GV, :, lanes] = gvel
            outs[O_GN, :, lanes] = state[GA, :, lanes] - global_rate * (
                gmean + global_mu * gvel
            )
        for i in (O_RV, O_GV, O_GN):
            stores[i].start()
            drains.append(stores[i].wait)

    scale = 1.0 / math.sqrt(DW)

    def kcopy(h):
        return remote(ksend.at[h], krec.at[h], k_sem.at[h], k_sem.at[2 + h], other)

    def finish(h, theirs, ours):
        ksend[h] = (theirs * scale).astype(BF)
        go(kcopy(h))
        keys[:, pl.ds(pl.multiple_of((2 * h + r) * LB, LB), LB)] = (
            ours * scale
        ).astype(BF)

    def project0():
        rhs = wfull[0].reshape(DW, LB)
        finish(
            0,
            jnp.dot(act[1], rhs, preferred_element_type=F32),
            jnp.dot(act[0], rhs, preferred_element_type=F32),
        )

    def project1():
        theirs = ours = 0.0
        for i in (None, 0, 1, 2):
            if i is not None:
                for c, at in pieces:
                    z1recv(c, at, i).wait_recv()
            q = near((0, 1, -1, 2)[0 if i is None else i + 1])
            rhs = wfull[1, q].reshape(640, LB)
            span = pl.ds(pl.multiple_of(q * 640, LB), 640)
            theirs += jnp.dot(act[1, :, span], rhs, preferred_element_type=F32)
            ours += jnp.dot(act[0, :, span], rhs, preferred_element_type=F32)
        finish(1, theirs, ours)

    act_copy = remote(act.at[0], act.at[1], act_sem.at[0], act_sem.at[1], other)
    for h in (1, 0):
        rhs = cot[:, h * 256 : (h + 1) * 256]
        for q in range(N_ZL):
            lhs = act[0, :, q * 640 : (q + 1) * 640]
            term = lax.dot_general(
                lhs, rhs, (((0,), (0,)), ((), ())), preferred_element_type=F32
            ).astype(BF)
            for b in range(2):
                for t in range(N_Y):
                    part[2 * h + b, t, q] = term[
                        t * ROWS : (t + 1) * ROWS, b * LB : (b + 1) * LB
                    ]
        if h == 1:
            pl.semaphore_wait(barrier, len(peers))
            for k in (1, 2, 3):
                go(fsend(k))
            ystart(2)
        else:
            ystart(0)
            ystart(1)
    go(act_copy)
    for s in range(2):
        for lb in (2, 0, 1):
            ystep(lb, s)
    far()
    for lb in (2, 0, 1):
        ystep(lb, 2)
    ystep(3, 0)
    for lb in (2, 0, 1):
        ystep(lb, 3)
        yfinal(lb)
    for c in loads[2:]:
        c.wait()
    ystep(3, 1)
    adam(2)
    ystep(3, 2)
    adam(0)
    adam(1)
    ystep(3, 3)
    adam(3)
    for i in (O_FIRST, O_SECOND):
        stores[i].start()
        drains.append(stores[i].wait)
    for stage in (owner_a, owner_b, owner_c):
        for h in range(2):
            stage(h)
    wx(0)
    for j in (1, 2, 3):
        go(z0send(j))
    y0start(0)
    wx(1)
    y1start()
    y1step(0)
    y0step(0, 0)
    for j in (1, 2, 3):
        y0start(j)
    y1step(1)
    for s in range(3):
        y0step(0, s + 1)
        for j in (1, 2, 3):
            y0step(j, s)
        if s < 2:
            y1step(s + 2)
    replicated()
    for j in (1, 2, 3):
        y0step(j, 3)
    act_copy.wait_recv()
    project0()
    project1()
    for h in range(2):
        kcopy(h).wait_recv()
        keys[:, pl.ds(pl.multiple_of((2 * h + 1 - r) * LB, LB), LB)] = krec[h]
    k_store = pltpu.make_async_copy(keys, okeys_hbm, out_sem.at[5])
    k_store.start()
    for drain in drains:
        drain()
    for k in (1, 2):
        tsend(k).wait_send()
    gsend().wait_send()
    for k in (1, 2, 3):
        msend(k).wait_send()

    @pl.when(lax.rem(x, 2) == r)
    def _():
        for k in (1, 2, 3):
            wxsend(0, k).wait_send()

    k_store.wait()


def hand_over(*refs):
    sem = refs[18]
    loads = [
        pltpu.make_async_copy(refs[i], refs[12 + i], sem.at[0, i]) for i in range(6)
    ]
    stores = [
        pltpu.make_async_copy(refs[12 + i], refs[6 + i], sem.at[1, i]) for i in range(6)
    ]
    for c in loads:
        c.start()
    for c, o in zip(loads, stores):
        c.wait()
        o.start()
    for o in stores:
        o.wait()


def body(act, cot, w, m, v, ra, rm, ga, gm):
    dma = pltpu.SemaphoreType.DMA
    flat = lambda a: a.reshape(ROWS, KV)
    out = pl.pallas_call(
        kernel,
        out_shape=[jax.ShapeDtypeStruct((ROWS, KV), F32)] * 5
        + [jax.ShapeDtypeStruct((TOK, KV), BF)],
        in_specs=[pl.BlockSpec(memory_space=pl.ANY)] * 9,
        out_specs=[pl.BlockSpec(memory_space=pl.ANY)] * 6,
        scratch_shapes=[
            pltpu.VMEM((2, TOK, DW), BF),
            pltpu.VMEM((TOK, KV), BF),
            pltpu.VMEM((7, ROWS, KV), F32),
            pltpu.VMEM((4, N_Y, N_ZL, ROWS, LB), BF),
            pltpu.VMEM((2, 3, 4, N_ZL, ROWS, LB), BF),
            pltpu.VMEM((3, N_ZL, ROWS, LB), BF),
            pltpu.VMEM((3, N_ZL, ROWS, LB), BF),
            pltpu.VMEM((3, N_Y, ROWS, LB), BF),
            pltpu.VMEM((N_Y, ROWS, LB), BF),
            pltpu.VMEM((2, 4, ROWS, LB), BF),
            pltpu.VMEM((4, ROWS, LB), BF),
            pltpu.VMEM((N_X, ROWS, LB), BF),
            pltpu.VMEM((N_ZH, ROWS, LB), F32),
            pltpu.VMEM((2, ROWS, LB), F32),
            pltpu.VMEM((N_X, 2, ROWS, LB), F32),
            pltpu.VMEM((2, N_ZL, N_Y, ROWS, LB), BF),
            pltpu.VMEM((2, TOK, LB), BF),
            pltpu.VMEM((2, TOK, LB), BF),
            pltpu.VMEM((5, ROWS, KV), F32),
            pltpu.VMEM((TOK, KV), BF),
            dma((9,)),
            dma((6,)),
            dma((2,)),
            dma((2, 4, 4)),
            dma((2, 4, 4)),
            dma((3, 3)),
            dma((3, 3)),
            dma((3,)),
            dma((3,)),
            dma((4,)),
            dma((4,)),
            dma((2,)),
            dma((2,)),
            dma((2,)),
            dma((3,)),
            dma((4,)),
            dma((3,)),
            dma((2,)),
            dma((3,)),
            dma((3,)),
            dma((2, 4, 4)),
            dma((2, 4, 4)),
            dma((2, 4)),
            dma((2, 4)),
            dma((8, 3)),
            dma((8, 3)),
            dma((4,)),
        ],
        compiler_params=pltpu.CompilerParams(
            collective_id=0, has_side_effects=True, vmem_limit_bytes=60 * 1024 * 1024
        ),
        name="outer_sync",
    )(act, cot, *map(flat, (w, m, v, ra, rm, ga, gm)))
    first, second, rv, gv, gn, keys = pl.pallas_call(
        hand_over,
        out_shape=[jax.ShapeDtypeStruct(o.shape, o.dtype) for o in out],
        in_specs=[pl.BlockSpec(memory_space=pl.ANY)] * 6,
        out_specs=[pl.BlockSpec(memory_space=pl.ANY)] * 6,
        scratch_shapes=[pltpu.VMEM(o.shape, o.dtype) for o in out] + [dma((2, 6))],
        compiler_params=pltpu.CompilerParams(vmem_limit_bytes=60 * 1024 * 1024),
        name="hand_over",
    )(*out)
    return (
        first.reshape(1, 1, ROWS, KV),
        second.reshape(1, 1, ROWS, KV),
        rv.reshape(1, ROWS, KV),
        gv,
        gn,
        keys,
    )


def solution(mesh):
    finer = Mesh(
        mesh.devices.reshape(2, N_ZH, N_X, N_ZL, N_Y), ("region", "zh", "x", "zl", "y")
    )
    island = ("zh", "x")
    dev = ("zl", "y")
    every = ("region", "zh", "x", "zl", "y")
    return jax.shard_map(
        body,
        mesh=finer,
        in_specs=(
            P(every, None),
            P(every, None),
            P("region", island, dev, None),
            P("region", island, dev, None),
            P("region", island, dev, None),
            P("region", dev, None),
            P("region", dev, None),
            P(dev, None),
            P(dev, None),
        ),
        out_specs=(
            P("region", island, dev, None),
            P("region", island, dev, None),
            P("region", dev, None),
            P(dev, None),
            P(dev, None),
            P(every, None),
        ),
        check_vma=False,
    )
```

```python
import functools
import math

import jax
import jax.numpy as jnp
from jax import lax
from jax.experimental import pallas as pl
from jax.experimental.pallas import tpu as pltpu
from jax.sharding import Mesh
from jax.sharding import PartitionSpec as P

DW = 2560
KV = 512
TOK = 256
ROWS = 80
LB = 128
N_Y = 8
N_ZL = 4
N_ZH = 3
N_X = 4
MESH = pl.DeviceIdType.MESH
BF = jnp.bfloat16
F32 = jnp.float32

beta_first = 0.9
beta_second = 0.999
adam_eps = 1e-08
inner_rate = 0.05
weight_decay = 0.1
region_mu = 0.9
region_rate = 0.7
global_mu = 0.9
global_rate = 0.7

W_, M_, V_, RA, RM, GA, GM = range(7)
O_FIRST, O_SECOND, O_RV, O_GV, O_GN = range(5)
SIGN = (1, -1)


def hops(d, lb):
    return 4 if (lb % 2 == 0) == (d == 0) else 3


def kernel(
    act_hbm, cot_hbm, w_hbm, m_hbm, v_hbm, ra_hbm, rm_hbm, ga_hbm, gm_hbm,
    of_hbm, os_hbm, orv_hbm, ogv_hbm, ogn_hbm, okeys_hbm,
    act, cot, state, part, yrec, ysum, zrec, zfar, ypart, yfar, delta, xrec, trec,
    gap, means, wfull, ksend, krec, outs, keys,
    in_sem, out_sem, act_sem, ys_sem, yr_sem, zs_sem, zr_sem, fs_sem, fr_sem,
    xs_sem, xr_sem, ts_sem, tr_sem, g_sem, ms_sem, mr_sem, wxs_sem, wxr_sem,
    wz0s_sem, wz0r_sem, wy0s_sem, wy0r_sem, wy1s_sem, wy1r_sem, wz1s_sem, wz1r_sem,
    k_sem,
):
    r = lax.axis_index("region")
    zh = lax.axis_index("zh")
    x = lax.axis_index("x")
    zl = lax.axis_index("zl")
    y = lax.axis_index("y")
    z = zh * 4 + zl
    other = {"region": 1 - r}

    def to_z(off):
        t = lax.rem(z + off + 12, 12)
        return {"zh": t // 4, "zl": lax.rem(t, 4)}

    def to_y(off):
        return {"y": lax.rem(y + off + N_Y, N_Y)}

    def to_x(off):
        return {"x": lax.rem(x + off + N_X, N_X)}

    def remote(src, dst, ssem, rsem, dev):
        return pltpu.make_async_remote_copy(
            src_ref=src, dst_ref=dst, send_sem=ssem, recv_sem=rsem,
            device_id=dev, device_id_type=MESH,
        )

    drains = []

    def go(c):
        c.start()
        drains.append(c.wait_send)

    def go_if(cond, make):
        @pl.when(cond)
        def _():
            make().start()

        def drain():
            @pl.when(cond)
            def _():
                make().wait_send()

        drains.append(drain)

    loads = [
        pltpu.make_async_copy(act_hbm, act.at[0], in_sem.at[0]),
        pltpu.make_async_copy(cot_hbm, cot, in_sem.at[1]),
    ]
    for i, ref in enumerate((w_hbm, m_hbm, v_hbm, ra_hbm, rm_hbm, ga_hbm, gm_hbm)):
        loads.append(pltpu.make_async_copy(ref, state.at[i], in_sem.at[2 + i]))
    for c in loads:
        c.start()
    stores = [
        pltpu.make_async_copy(outs.at[i], o, out_sem.at[i])
        for i, o in enumerate((of_hbm, os_hbm, orv_hbm, ogv_hbm, ogn_hbm))
    ]

    barrier = pltpu.get_barrier_semaphore()
    peers = [other] + [to_y(k) for k in (1, -1)] + [to_x(k) for k in (1, 2, 3)]
    peers += [to_z(k) for k in (-4, -3, -2, -1, 1, 2, 3, 4)]
    for dev in peers:
        pl.semaphore_signal(barrier, inc=1, device_id=dev, device_id_type=MESH)

    loads[0].wait()
    loads[1].wait()

    def ysend(d, lb, s):
        t = lax.rem(y + SIGN[d] * (hops(d, lb) - s) + N_Y, N_Y)
        if lb == 3:
            src = ypart.at[t] if s == 0 else yfar.at[d, s - 1]
            dst = yfar.at[d, s]
        else:
            src = part.at[lb, t] if s == 0 else yrec.at[d, lb, s - 1]
            dst = yrec.at[d, lb, s]
        return remote(
            src, dst, ys_sem.at[d, lb, s], yr_sem.at[d, lb, s], to_y(SIGN[d])
        )

    def ystart(lb):
        for d in range(2):
            go(ysend(d, lb, 0))

    def ystep(lb, s):
        for d in range(2):
            n = hops(d, lb)
            if s >= n:
                continue
            ysend(d, lb, s).wait_recv()
            if s < n - 1:
                t = lax.rem(y + SIGN[d] * (n - s - 1) + N_Y, N_Y)
                if lb == 3:
                    yfar[d, s] = (
                        yfar[d, s].astype(F32) + ypart[t].astype(F32)
                    ).astype(BF)
                else:
                    yrec[d, lb, s] = (
                        yrec[d, lb, s].astype(F32) + part[lb, t].astype(F32)
                    ).astype(BF)
                go(ysend(d, lb, s + 1))

    def zsend(lb, k):
        t = lax.rem(zl + k, N_ZL)
        return remote(
            ysum.at[lb, t], zrec.at[lb, zl], zs_sem.at[lb, k - 1],
            zr_sem.at[lb, k - 1], {"zl": t},
        )

    def zrecv(lb, k):
        src = lax.rem(zl + N_ZL - k, N_ZL)
        return remote(
            ysum.at[lb, zl], zrec.at[lb, src], zs_sem.at[lb, k - 1],
            zr_sem.at[lb, k - 1], {"zl": src},
        )

    def yfinal(lb):
        total = (
            part[lb, y].astype(F32)
            + yrec[0, lb, hops(0, lb) - 1].astype(F32)
            + yrec[1, lb, hops(1, lb) - 1].astype(F32)
        )
        ysum[lb] = total.astype(BF)
        for k in (1, 2, 3):
            go(zsend(lb, k))

    def fsend(k):
        t = lax.rem(zl + k, N_ZL)
        return remote(
            part.at[3, :, t], zfar.at[k - 1], fs_sem.at[k - 1], fr_sem.at[k - 1],
            {"zl": t},
        )

    def far():
        for k in (1, 2, 3):
            fsend(k).wait_recv()
        for t in range(N_Y):
            total = part[3, t, zl].astype(F32)
            for k in range(3):
                total = total + zfar[k, t].astype(F32)
            ypart[t] = total.astype(BF)
        ystart(3)

    def xsend(lb):
        return remote(
            delta.at[lb], xrec.at[x], xs_sem.at[lb], xr_sem.at[x], {"x": lb}
        )

    def adam(lb):
        if lb == 3:
            g = (
                ypart[y].astype(F32)
                + yfar[0, hops(0, 3) - 1].astype(F32)
                + yfar[1, hops(1, 3) - 1].astype(F32)
            )
        else:
            for k in (1, 2, 3):
                zrecv(lb, k).wait_recv()
            g = ysum[lb, zl].astype(F32)
            for k in (1, 2, 3):
                g = g + zrec[lb, lax.rem(zl + k, N_ZL)].astype(F32)
        lanes = slice(lb * LB, (lb + 1) * LB)
        gradient = g * (1.0 / math.sqrt(TOK * 32))
        first = beta_first * state[M_, :, lanes] + (1.0 - beta_first) * gradient
        second = (
            beta_second * state[V_, :, lanes]
            + (1.0 - beta_second) * gradient * gradient
        )
        weight = state[W_, :, lanes]
        inner = weight - inner_rate * (
            first / (jnp.sqrt(second) + adam_eps) + weight_decay * weight
        )
        outs[O_FIRST, :, lanes] = first
        outs[O_SECOND, :, lanes] = second
        delta[lb] = (state[RA, :, lanes] - inner).astype(BF)
        go_if(x != lb, lambda: xsend(lb))

    mine = pl.ds(pl.multiple_of(x * LB, LB), LB)

    def tsend(k):
        return remote(
            trec.at[zh], trec.at[zh], ts_sem.at[k - 1], tr_sem.at[k - 1],
            {"zh": lax.rem(zh + k, N_ZH)},
        )

    def trecv(k):
        src = lax.rem(zh + N_ZH - k, N_ZH)
        return remote(
            trec.at[zh], trec.at[src], ts_sem.at[k - 1], tr_sem.at[k - 1], {"zh": src}
        )

    def gsend():
        return remote(gap.at[r], gap.at[r], g_sem.at[0], g_sem.at[1], other)

    def owner_a(h):
        @pl.when(x // 2 == h)
        def _():
            t = delta[x].astype(F32)
            for k in (1, 2, 3):
                src = lax.rem(x + k, N_X)
                remote(
                    delta.at[0], xrec.at[src], xs_sem.at[0], xr_sem.at[src], {"x": src}
                ).wait_recv()
                t = t + xrec[src].astype(F32)
            trec[zh] = t
            for k in (1, 2):
                tsend(k).start()

    def owner_b(h):
        @pl.when(x // 2 == h)
        def _():
            for k in (1, 2):
                trecv(k).wait_recv()
            region_mean = ((trec[0] + trec[1]) + trec[2]) / 12
            region_velocity = region_mu * state[RM, :, mine] + region_mean
            region_params = state[RA, :, mine] - region_rate * (
                region_mean + region_mu * region_velocity
            )
            gap[r] = state[GA, :, mine] - region_params
            gsend().start()
            means[x, 0] = region_mean

    def wxsend(h, k):
        slot = wfull.at[h, zl, y]
        return remote(slot, slot, wxs_sem.at[k - 1], wxr_sem.at[h], to_x(k))

    def msend(k):
        return remote(
            means.at[x], means.at[x], ms_sem.at[k - 1], mr_sem.at[x], to_x(k)
        )

    def owner_c(h):
        @pl.when(x // 2 == h)
        def _():
            remote(
                gap.at[r], gap.at[1 - r], g_sem.at[0], g_sem.at[1], other
            ).wait_recv()
            global_mean = (gap[0] + gap[1]) / 2
            global_velocity = global_mu * state[GM, :, mine] + global_mean
            global_new = state[GA, :, mine] - global_rate * (
                global_mean + global_mu * global_velocity
            )

            @pl.when(lax.rem(x, 2) == r)
            def _():
                wfull[h, zl, y] = global_new.astype(BF)
                for k in (1, 2, 3):
                    wxsend(h, k).start()

            means[x, 1] = global_mean

    def wx(h):
        @pl.when(x != 2 * h + r)
        def _():
            slot = wfull.at[h, zl, y]
            remote(
                slot, slot, wxs_sem.at[0], wxr_sem.at[h], {"x": 2 * h + r}
            ).wait_recv()

    def near(off):
        return lax.rem(zl - off + N_ZL, N_ZL)

    def origin(d, s):
        return lax.rem(y - SIGN[d] * s + N_Y, N_Y)

    offs = (0, 1, -1, 2)

    def z0(j, off):
        slot = wfull.at[0, near(off), y]
        return slot, wz0s_sem.at[j - 1], wz0r_sem.at[j - 1]

    def z0send(j):
        slot, ssem, rsem = z0(j, 0)
        return remote(slot, slot, ssem, rsem, to_z(offs[j]))

    def z0recv(j):
        slot, ssem, rsem = z0(j, offs[j])
        return remote(slot, slot, ssem, rsem, to_z(-offs[j]))

    def y0send(d, j, s):
        slot = wfull.at[0, near(offs[j]), origin(d, s)]
        return remote(
            slot, slot, wy0s_sem.at[d, j, s], wy0r_sem.at[d, j, s], to_y(SIGN[d])
        )

    def y0recv(d, j, s):
        slot = wfull.at[0, near(offs[j]), origin(d, s + 1)]
        return remote(
            slot, slot, wy0s_sem.at[d, j, s], wy0r_sem.at[d, j, s], to_y(-SIGN[d])
        )

    def y0start(j):
        if j > 0:
            z0recv(j).wait_recv()
        for d in range(2):
            go(y0send(d, j, 0))

    def y0step(j, s):
        for d in range(2):
            if s < hops(d, j):
                y0recv(d, j, s).wait_recv()
                if s + 1 < hops(d, j):
                    go(y0send(d, j, s + 1))

    def y1(d, s, at):
        slot = wfull.at[1, zl, origin(d, at)]
        return slot, slot, wy1s_sem.at[d, s], wy1r_sem.at[d, s]

    def z1off(c, i):
        return (1, -1, 2 if c % 2 == 0 else -2)[i]

    def z1send(c, at, i):
        slot = wfull.at[1, zl, at]
        return remote(
            slot, slot, wz1s_sem.at[c, i], wz1r_sem.at[c, i], to_z(z1off(c, i))
        )

    def z1recv(c, at, i):
        slot = wfull.at[1, near(z1off(c, i)), at]
        return remote(
            slot, slot, wz1s_sem.at[c, i], wz1r_sem.at[c, i], to_z(-z1off(c, i))
        )

    pieces = [(0, y)]

    def y1start():
        for d in range(2):
            go(remote(*y1(d, 0, 0), to_y(SIGN[d])))
        for i in range(3):
            go(z1send(0, y, i))

    def y1step(s):
        for d in range(2):
            n = hops(d, 0)
            if s < n:
                remote(*y1(d, s, s + 1), to_y(-SIGN[d])).wait_recv()
                if s + 1 < n:
                    go(remote(*y1(d, s + 1, s + 1), to_y(SIGN[d])))
                c, at = len(pieces), origin(d, s + 1)
                pieces.append((c, at))
                for i in (2, 0, 1):
                    go(z1send(c, at, i))

    def replicated():
        for lb in range(4):
            @pl.when(x != lb)
            def _():
                remote(
                    means.at[x], means.at[lb], ms_sem.at[0], mr_sem.at[lb], {"x": lb}
                ).wait_recv()

            lanes = slice(lb * LB, (lb + 1) * LB)
            rmean = means[lb, 0]
            gmean = means[lb, 1]
            outs[O_RV, :, lanes] = region_mu * state[RM, :, lanes] + rmean
            gvel = global_mu * state[GM, :, lanes] + gmean
            outs[O_GV, :, lanes] = gvel
            outs[O_GN, :, lanes] = state[GA, :, lanes] - global_rate * (
                gmean + global_mu * gvel
            )
        for i in (O_RV, O_GV, O_GN):
            stores[i].start()
            drains.append(stores[i].wait)

    scale = 1.0 / math.sqrt(DW)

    def kcopy(h):
        return remote(ksend.at[h], krec.at[h], k_sem.at[h], k_sem.at[2 + h], other)

    def finish(h, theirs, ours):
        ksend[h] = (theirs * scale).astype(BF)
        go(kcopy(h))
        keys[:, pl.ds(pl.multiple_of((2 * h + r) * LB, LB), LB)] = (
            ours * scale
        ).astype(BF)

    def slab(h, j):
        q = near(offs[j])
        rhs = wfull[h, q].reshape(640, LB)
        span = pl.ds(pl.multiple_of(q * 640, LB), 640)
        return (
            jnp.dot(act[1, :, span], rhs, preferred_element_type=F32),
            jnp.dot(act[0, :, span], rhs, preferred_element_type=F32),
        )

    def project(h, ready):
        theirs, ours = slab(h, 0)
        for j in (1, 2, 3):
            ready(j)
            more = slab(h, j)
            theirs, ours = theirs + more[0], ours + more[1]
        finish(h, theirs, ours)

    def ready0(j):
        y0step(j, 3)

    def ready1(j):
        for c, at in pieces:
            z1recv(c, at, j - 1).wait_recv()

    act_copy = remote(act.at[0], act.at[1], act_sem.at[0], act_sem.at[1], other)
    for h in (1, 0):
        rhs = cot[:, h * 256 : (h + 1) * 256]
        for q in range(N_ZL):
            lhs = act[0, :, q * 640 : (q + 1) * 640]
            term = lax.dot_general(
                lhs, rhs, (((0,), (0,)), ((), ())), preferred_element_type=F32
            ).astype(BF)
            for b in range(2):
                for t in range(N_Y):
                    part[2 * h + b, t, q] = term[
                        t * ROWS : (t + 1) * ROWS, b * LB : (b + 1) * LB
                    ]
        if h == 1:
            pl.semaphore_wait(barrier, len(peers))
            for k in (1, 2, 3):
                go(fsend(k))
            ystart(2)
        else:
            ystart(0)
            ystart(1)
    go(act_copy)
    for s in range(2):
        for lb in (2, 0, 1):
            ystep(lb, s)
    far()
    for lb in (2, 0, 1):
        ystep(lb, 2)
    ystep(3, 0)
    for lb in (2, 0, 1):
        ystep(lb, 3)
        yfinal(lb)
    for c in loads[2:]:
        c.wait()
    ystep(3, 1)
    adam(2)
    ystep(3, 2)
    adam(0)
    adam(1)
    ystep(3, 3)
    adam(3)
    for i in (O_FIRST, O_SECOND):
        stores[i].start()
        drains.append(stores[i].wait)
    for stage in (owner_a, owner_b, owner_c):
        for h in range(2):
            stage(h)
    wx(0)
    for j in (1, 2, 3):
        go(z0send(j))
    y0start(0)
    wx(1)
    y1start()
    for k in (1, 2, 3):
        msend(k).start()
    y1step(0)
    y0step(0, 0)
    for j in (1, 2, 3):
        y0start(j)
    y1step(1)
    for s in range(3):
        y0step(0, s + 1)
        for j in (1, 2, 3):
            y0step(j, s)
        if s < 2:
            y1step(s + 2)
    replicated()
    act_copy.wait_recv()
    project(1, ready1)
    project(0, ready0)
    for h in (1, 0):
        kcopy(h).wait_recv()
        keys[:, pl.ds(pl.multiple_of((2 * h + 1 - r) * LB, LB), LB)] = krec[h]
    k_store = pltpu.make_async_copy(keys, okeys_hbm, out_sem.at[5])
    k_store.start()
    for drain in drains:
        drain()
    for k in (1, 2):
        tsend(k).wait_send()
    gsend().wait_send()
    for k in (1, 2, 3):
        msend(k).wait_send()

    @pl.when(lax.rem(x, 2) == r)
    def _():
        for k in (1, 2, 3):
            wxsend(0, k).wait_send()

    k_store.wait()


def hand_over(*refs):
    sem = refs[18]
    loads = [
        pltpu.make_async_copy(refs[i], refs[12 + i], sem.at[0, i]) for i in range(6)
    ]
    stores = [
        pltpu.make_async_copy(refs[12 + i], refs[6 + i], sem.at[1, i]) for i in range(6)
    ]
    for c in loads:
        c.start()
    for c, o in zip(loads, stores):
        c.wait()
        o.start()
    for o in stores:
        o.wait()


def body(act, cot, w, m, v, ra, rm, ga, gm):
    dma = pltpu.SemaphoreType.DMA
    flat = lambda a: a.reshape(ROWS, KV)
    out = pl.pallas_call(
        kernel,
        out_shape=[jax.ShapeDtypeStruct((ROWS, KV), F32)] * 5
        + [jax.ShapeDtypeStruct((TOK, KV), BF)],
        in_specs=[pl.BlockSpec(memory_space=pl.ANY)] * 9,
        out_specs=[pl.BlockSpec(memory_space=pl.ANY)] * 6,
        scratch_shapes=[
            pltpu.VMEM((2, TOK, DW), BF),
            pltpu.VMEM((TOK, KV), BF),
            pltpu.VMEM((7, ROWS, KV), F32),
            pltpu.VMEM((4, N_Y, N_ZL, ROWS, LB), BF),
            pltpu.VMEM((2, 3, 4, N_ZL, ROWS, LB), BF),
            pltpu.VMEM((3, N_ZL, ROWS, LB), BF),
            pltpu.VMEM((3, N_ZL, ROWS, LB), BF),
            pltpu.VMEM((3, N_Y, ROWS, LB), BF),
            pltpu.VMEM((N_Y, ROWS, LB), BF),
            pltpu.VMEM((2, 4, ROWS, LB), BF),
            pltpu.VMEM((4, ROWS, LB), BF),
            pltpu.VMEM((N_X, ROWS, LB), BF),
            pltpu.VMEM((N_ZH, ROWS, LB), F32),
            pltpu.VMEM((2, ROWS, LB), F32),
            pltpu.VMEM((N_X, 2, ROWS, LB), F32),
            pltpu.VMEM((2, N_ZL, N_Y, ROWS, LB), BF),
            pltpu.VMEM((2, TOK, LB), BF),
            pltpu.VMEM((2, TOK, LB), BF),
            pltpu.VMEM((5, ROWS, KV), F32),
            pltpu.VMEM((TOK, KV), BF),
            dma((9,)),
            dma((6,)),
            dma((2,)),
            dma((2, 4, 4)),
            dma((2, 4, 4)),
            dma((3, 3)),
            dma((3, 3)),
            dma((3,)),
            dma((3,)),
            dma((4,)),
            dma((4,)),
            dma((2,)),
            dma((2,)),
            dma((2,)),
            dma((3,)),
            dma((4,)),
            dma((3,)),
            dma((2,)),
            dma((3,)),
            dma((3,)),
            dma((2, 4, 4)),
            dma((2, 4, 4)),
            dma((2, 4)),
            dma((2, 4)),
            dma((8, 3)),
            dma((8, 3)),
            dma((4,)),
        ],
        compiler_params=pltpu.CompilerParams(
            collective_id=0, has_side_effects=True, vmem_limit_bytes=60 * 1024 * 1024
        ),
        name="outer_sync",
    )(act, cot, *map(flat, (w, m, v, ra, rm, ga, gm)))
    first, second, rv, gv, gn, keys = pl.pallas_call(
        hand_over,
        out_shape=[jax.ShapeDtypeStruct(o.shape, o.dtype) for o in out],
        in_specs=[pl.BlockSpec(memory_space=pl.ANY)] * 6,
        out_specs=[pl.BlockSpec(memory_space=pl.ANY)] * 6,
        scratch_shapes=[pltpu.VMEM(o.shape, o.dtype) for o in out] + [dma((2, 6))],
        compiler_params=pltpu.CompilerParams(vmem_limit_bytes=60 * 1024 * 1024),
        name="hand_over",
    )(*out)
    return (
        first.reshape(1, 1, ROWS, KV),
        second.reshape(1, 1, ROWS, KV),
        rv.reshape(1, ROWS, KV),
        gv,
        gn,
        keys,
    )


def solution(mesh):
    finer = Mesh(
        mesh.devices.reshape(2, N_ZH, N_X, N_ZL, N_Y), ("region", "zh", "x", "zl", "y")
    )
    island = ("zh", "x")
    dev = ("zl", "y")
    every = ("region", "zh", "x", "zl", "y")
    return jax.shard_map(
        body,
        mesh=finer,
        in_specs=(
            P(every, None),
            P(every, None),
            P("region", island, dev, None),
            P("region", island, dev, None),
            P("region", island, dev, None),
            P("region", dev, None),
            P("region", dev, None),
            P(dev, None),
            P(dev, None),
        ),
        out_specs=(
            P("region", island, dev, None),
            P("region", island, dev, None),
            P("region", dev, None),
            P(dev, None),
            P(dev, None),
            P(every, None),
        ),
        check_vma=False,
    )
```

```python
import functools
import math

import jax
import jax.numpy as jnp
from jax import lax
from jax.experimental import pallas as pl
from jax.experimental.pallas import tpu as pltpu
from jax.sharding import Mesh
from jax.sharding import PartitionSpec as P

DW = 2560
KV = 512
TOK = 256
ROWS = 80
LB = 128
N_Y = 8
N_ZL = 4
N_ZH = 3
N_X = 4
MESH = pl.DeviceIdType.MESH
BF = jnp.bfloat16
F32 = jnp.float32

beta_first = 0.9
beta_second = 0.999
adam_eps = 1e-08
inner_rate = 0.05
weight_decay = 0.1
region_mu = 0.9
region_rate = 0.7
global_mu = 0.9
global_rate = 0.7

W_, M_, V_, RA, RM, GA, GM = range(7)
O_FIRST, O_SECOND, O_RV, O_GV, O_GN = range(5)
SIGN = (1, -1)


def hops(d, lb):
    return 4 if (lb % 2 == 0) == (d == 0) else 3


def kernel(
    act_hbm, cot_hbm, w_hbm, m_hbm, v_hbm, ra_hbm, rm_hbm, ga_hbm, gm_hbm,
    of_hbm, os_hbm, orv_hbm, ogv_hbm, ogn_hbm, okeys_hbm,
    act, cot, state, part, yrec, ysum, zrec, zfar, ypart, yfar, delta, xrec, trec,
    gap, means, wfull, ksend, krec, outs, keys,
    in_sem, out_sem, act_sem, ys_sem, yr_sem, zs_sem, zr_sem, fs_sem, fr_sem,
    xs_sem, xr_sem, ts_sem, tr_sem, g_sem, ms_sem, mr_sem, wxs_sem, wxr_sem,
    wz0s_sem, wz0r_sem, wy0s_sem, wy0r_sem, wy1s_sem, wy1r_sem, wz1s_sem, wz1r_sem,
    k_sem,
):
    r = lax.axis_index("region")
    zh = lax.axis_index("zh")
    x = lax.axis_index("x")
    zl = lax.axis_index("zl")
    y = lax.axis_index("y")
    z = zh * 4 + zl
    other = {"region": 1 - r}

    def to_z(off):
        t = lax.rem(z + off + 12, 12)
        return {"zh": t // 4, "zl": lax.rem(t, 4)}

    def to_y(off):
        return {"y": lax.rem(y + off + N_Y, N_Y)}

    def to_x(off):
        return {"x": lax.rem(x + off + N_X, N_X)}

    def remote(src, dst, ssem, rsem, dev):
        return pltpu.make_async_remote_copy(
            src_ref=src, dst_ref=dst, send_sem=ssem, recv_sem=rsem,
            device_id=dev, device_id_type=MESH,
        )

    drains = []

    def go(c):
        c.start()
        drains.append(c.wait_send)

    def go_if(cond, make):
        @pl.when(cond)
        def _():
            make().start()

        def drain():
            @pl.when(cond)
            def _():
                make().wait_send()

        drains.append(drain)

    loads = [
        pltpu.make_async_copy(act_hbm, act.at[0], in_sem.at[0]),
        pltpu.make_async_copy(cot_hbm, cot, in_sem.at[1]),
    ]
    for i, ref in enumerate((w_hbm, m_hbm, v_hbm, ra_hbm, rm_hbm, ga_hbm, gm_hbm)):
        loads.append(pltpu.make_async_copy(ref, state.at[i], in_sem.at[2 + i]))
    for c in loads:
        c.start()
    stores = [
        pltpu.make_async_copy(outs.at[i], o, out_sem.at[i])
        for i, o in enumerate((of_hbm, os_hbm, orv_hbm, ogv_hbm, ogn_hbm))
    ]

    barrier = pltpu.get_barrier_semaphore()
    peers = [other] + [to_y(k) for k in (1, -1)] + [to_x(k) for k in (1, 2, 3)]
    peers += [to_z(k) for k in (-4, -3, -2, -1, 1, 2, 3, 4)]
    for dev in peers:
        pl.semaphore_signal(barrier, inc=1, device_id=dev, device_id_type=MESH)

    loads[0].wait()
    loads[1].wait()

    def ysend(d, lb, s):
        t = lax.rem(y + SIGN[d] * (hops(d, lb) - s) + N_Y, N_Y)
        if lb == 3:
            src = ypart.at[t] if s == 0 else yfar.at[d, s - 1]
            dst = yfar.at[d, s]
        else:
            src = part.at[lb, t] if s == 0 else yrec.at[d, lb, s - 1]
            dst = yrec.at[d, lb, s]
        return remote(
            src, dst, ys_sem.at[d, lb, s], yr_sem.at[d, lb, s], to_y(SIGN[d])
        )

    def ystart(lb):
        for d in range(2):
            go(ysend(d, lb, 0))

    def ystep(lb, s):
        for d in range(2):
            n = hops(d, lb)
            if s >= n:
                continue
            ysend(d, lb, s).wait_recv()
            if s < n - 1:
                t = lax.rem(y + SIGN[d] * (n - s - 1) + N_Y, N_Y)
                if lb == 3:
                    yfar[d, s] = (
                        yfar[d, s].astype(F32) + ypart[t].astype(F32)
                    ).astype(BF)
                else:
                    yrec[d, lb, s] = (
                        yrec[d, lb, s].astype(F32) + part[lb, t].astype(F32)
                    ).astype(BF)
                go(ysend(d, lb, s + 1))

    def zsend(lb, k):
        t = lax.rem(zl + k, N_ZL)
        return remote(
            ysum.at[lb, t], zrec.at[lb, zl], zs_sem.at[lb, k - 1],
            zr_sem.at[lb, k - 1], {"zl": t},
        )

    def zrecv(lb, k):
        src = lax.rem(zl + N_ZL - k, N_ZL)
        return remote(
            ysum.at[lb, zl], zrec.at[lb, src], zs_sem.at[lb, k - 1],
            zr_sem.at[lb, k - 1], {"zl": src},
        )

    def yfinal(lb):
        total = (
            part[lb, y].astype(F32)
            + yrec[0, lb, hops(0, lb) - 1].astype(F32)
            + yrec[1, lb, hops(1, lb) - 1].astype(F32)
        )
        ysum[lb] = total.astype(BF)
        for k in (1, 2, 3):
            go(zsend(lb, k))

    def fsend(k):
        t = lax.rem(zl + k, N_ZL)
        return remote(
            part.at[3, :, t], zfar.at[k - 1], fs_sem.at[k - 1], fr_sem.at[k - 1],
            {"zl": t},
        )

    def far():
        for k in (1, 2, 3):
            fsend(k).wait_recv()
        for t in range(N_Y):
            total = part[3, t, zl].astype(F32)
            for k in range(3):
                total = total + zfar[k, t].astype(F32)
            ypart[t] = total.astype(BF)
        ystart(3)

    def xsend(lb):
        return remote(
            delta.at[lb], xrec.at[x], xs_sem.at[lb], xr_sem.at[x], {"x": lb}
        )

    def adam(lb):
        if lb == 3:
            g = (
                ypart[y].astype(F32)
                + yfar[0, hops(0, 3) - 1].astype(F32)
                + yfar[1, hops(1, 3) - 1].astype(F32)
            )
        else:
            for k in (1, 2, 3):
                zrecv(lb, k).wait_recv()
            g = ysum[lb, zl].astype(F32)
            for k in (1, 2, 3):
                g = g + zrec[lb, lax.rem(zl + k, N_ZL)].astype(F32)
        lanes = slice(lb * LB, (lb + 1) * LB)
        gradient = g * (1.0 / math.sqrt(TOK * 32))
        first = beta_first * state[M_, :, lanes] + (1.0 - beta_first) * gradient
        second = (
            beta_second * state[V_, :, lanes]
            + (1.0 - beta_second) * gradient * gradient
        )
        weight = state[W_, :, lanes]
        inner = weight - inner_rate * (
            first / (jnp.sqrt(second) + adam_eps) + weight_decay * weight
        )
        outs[O_FIRST, :, lanes] = first
        outs[O_SECOND, :, lanes] = second
        delta[lb] = state[RA, :, lanes] - inner
        go_if(x != lb, lambda: xsend(lb))

    mine = pl.ds(pl.multiple_of(x * LB, LB), LB)

    def tsend(k):
        return remote(
            trec.at[zh], trec.at[zh], ts_sem.at[k - 1], tr_sem.at[k - 1],
            {"zh": lax.rem(zh + k, N_ZH)},
        )

    def trecv(k):
        src = lax.rem(zh + N_ZH - k, N_ZH)
        return remote(
            trec.at[zh], trec.at[src], ts_sem.at[k - 1], tr_sem.at[k - 1], {"zh": src}
        )

    def gsend():
        return remote(gap.at[r], gap.at[r], g_sem.at[0], g_sem.at[1], other)

    def owner_a(h):
        @pl.when(x // 2 == h)
        def _():
            t = delta[x]
            for k in (1, 2, 3):
                src = lax.rem(x + k, N_X)
                remote(
                    delta.at[0], xrec.at[src], xs_sem.at[0], xr_sem.at[src], {"x": src}
                ).wait_recv()
                t = t + xrec[src]
            trec[zh] = t.astype(BF)
            for k in (1, 2):
                tsend(k).start()

    def owner_b(h):
        @pl.when(x // 2 == h)
        def _():
            for k in (1, 2):
                trecv(k).wait_recv()
            region_mean = (
                (trec[0].astype(F32) + trec[1].astype(F32)) + trec[2].astype(F32)
            ) / 12
            region_velocity = region_mu * state[RM, :, mine] + region_mean
            region_params = state[RA, :, mine] - region_rate * (
                region_mean + region_mu * region_velocity
            )
            gap[r] = state[GA, :, mine] - region_params
            gsend().start()
            means[x, 0] = region_mean

    def wxsend(h, k):
        slot = wfull.at[h, zl, y]
        return remote(slot, slot, wxs_sem.at[k - 1], wxr_sem.at[h], to_x(k))

    def msend(k):
        return remote(
            means.at[x], means.at[x], ms_sem.at[k - 1], mr_sem.at[x], to_x(k)
        )

    def owner_c(h):
        @pl.when(x // 2 == h)
        def _():
            remote(
                gap.at[r], gap.at[1 - r], g_sem.at[0], g_sem.at[1], other
            ).wait_recv()
            global_mean = (gap[0] + gap[1]) / 2
            global_velocity = global_mu * state[GM, :, mine] + global_mean
            global_new = state[GA, :, mine] - global_rate * (
                global_mean + global_mu * global_velocity
            )

            @pl.when(lax.rem(x, 2) == r)
            def _():
                wfull[h, zl, y] = global_new.astype(BF)
                for k in (1, 2, 3):
                    wxsend(h, k).start()

            means[x, 1] = global_mean
            for k in (1, 2, 3):
                msend(k).start()

    def wx(h):
        @pl.when(x != 2 * h + r)
        def _():
            slot = wfull.at[h, zl, y]
            remote(
                slot, slot, wxs_sem.at[0], wxr_sem.at[h], {"x": 2 * h + r}
            ).wait_recv()

    def near(off):
        return lax.rem(zl - off + N_ZL, N_ZL)

    def origin(d, s):
        return lax.rem(y - SIGN[d] * s + N_Y, N_Y)

    offs = (0, 1, -1, 2)

    def z0(j, off):
        slot = wfull.at[0, near(off), y]
        return slot, wz0s_sem.at[j - 1], wz0r_sem.at[j - 1]

    def z0send(j):
        slot, ssem, rsem = z0(j, 0)
        return remote(slot, slot, ssem, rsem, to_z(offs[j]))

    def z0recv(j):
        slot, ssem, rsem = z0(j, offs[j])
        return remote(slot, slot, ssem, rsem, to_z(-offs[j]))

    def y0send(d, j, s):
        slot = wfull.at[0, near(offs[j]), origin(d, s)]
        return remote(
            slot, slot, wy0s_sem.at[d, j, s], wy0r_sem.at[d, j, s], to_y(SIGN[d])
        )

    def y0recv(d, j, s):
        slot = wfull.at[0, near(offs[j]), origin(d, s + 1)]
        return remote(
            slot, slot, wy0s_sem.at[d, j, s], wy0r_sem.at[d, j, s], to_y(-SIGN[d])
        )

    def y0start(j):
        if j > 0:
            z0recv(j).wait_recv()
        for d in range(2):
            go(y0send(d, j, 0))

    def y0step(j, s):
        for d in range(2):
            if s < hops(d, j):
                y0recv(d, j, s).wait_recv()
                if s + 1 < hops(d, j):
                    go(y0send(d, j, s + 1))

    def y1(d, s, at):
        slot = wfull.at[1, zl, origin(d, at)]
        return slot, slot, wy1s_sem.at[d, s], wy1r_sem.at[d, s]

    def z1off(c, i):
        return (1, -1, 2 if c % 2 == 0 else -2)[i]

    def z1send(c, at, i):
        slot = wfull.at[1, zl, at]
        return remote(
            slot, slot, wz1s_sem.at[c, i], wz1r_sem.at[c, i], to_z(z1off(c, i))
        )

    def z1recv(c, at, i):
        slot = wfull.at[1, near(z1off(c, i)), at]
        return remote(
            slot, slot, wz1s_sem.at[c, i], wz1r_sem.at[c, i], to_z(-z1off(c, i))
        )

    pieces = [(0, y)]

    def y1start():
        for d in range(2):
            go(remote(*y1(d, 0, 0), to_y(SIGN[d])))
        for i in range(3):
            go(z1send(0, y, i))

    def y1step(s):
        for d in range(2):
            n = hops(d, 0)
            if s < n:
                remote(*y1(d, s, s + 1), to_y(-SIGN[d])).wait_recv()
                if s + 1 < n:
                    go(remote(*y1(d, s + 1, s + 1), to_y(SIGN[d])))
                c, at = len(pieces), origin(d, s + 1)
                pieces.append((c, at))
                for i in (2, 0, 1):
                    go(z1send(c, at, i))

    def replicated():
        for lb in range(4):
            @pl.when(x != lb)
            def _():
                remote(
                    means.at[x], means.at[lb], ms_sem.at[0], mr_sem.at[lb], {"x": lb}
                ).wait_recv()

            lanes = slice(lb * LB, (lb + 1) * LB)
            rmean = means[lb, 0]
            gmean = means[lb, 1]
            outs[O_RV, :, lanes] = region_mu * state[RM, :, lanes] + rmean
            gvel = global_mu * state[GM, :, lanes] + gmean
            outs[O_GV, :, lanes] = gvel
            outs[O_GN, :, lanes] = state[GA, :, lanes] - global_rate * (
                gmean + global_mu * gvel
            )
        for i in (O_RV, O_GV, O_GN):
            stores[i].start()
            drains.append(stores[i].wait)

    scale = 1.0 / math.sqrt(DW)

    def kcopy(h):
        return remote(ksend.at[h], krec.at[h], k_sem.at[h], k_sem.at[2 + h], other)

    def finish(h, theirs, ours):
        ksend[h] = (theirs * scale).astype(BF)
        go(kcopy(h))
        keys[:, pl.ds(pl.multiple_of((2 * h + r) * LB, LB), LB)] = (
            ours * scale
        ).astype(BF)

    def slab(h, j):
        q = near(offs[j])
        rhs = wfull[h, q].reshape(640, LB)
        span = pl.ds(pl.multiple_of(q * 640, LB), 640)
        return (
            jnp.dot(act[1, :, span], rhs, preferred_element_type=F32),
            jnp.dot(act[0, :, span], rhs, preferred_element_type=F32),
        )

    def project(h, ready):
        theirs, ours = slab(h, 0)
        for j in (1, 2, 3):
            ready(j)
            more = slab(h, j)
            theirs, ours = theirs + more[0], ours + more[1]
        finish(h, theirs, ours)

    def ready0(j):
        y0step(j, 3)

    def ready1(j):
        for c, at in pieces:
            z1recv(c, at, j - 1).wait_recv()

    act_copy = remote(act.at[0], act.at[1], act_sem.at[0], act_sem.at[1], other)
    for h in (1, 0):
        rhs = cot[:, h * 256 : (h + 1) * 256]
        for q in range(N_ZL):
            lhs = act[0, :, q * 640 : (q + 1) * 640]
            term = lax.dot_general(
                lhs, rhs, (((0,), (0,)), ((), ())), preferred_element_type=F32
            ).astype(BF)
            for b in range(2):
                for t in range(N_Y):
                    part[2 * h + b, t, q] = term[
                        t * ROWS : (t + 1) * ROWS, b * LB : (b + 1) * LB
                    ]
        if h == 1:
            pl.semaphore_wait(barrier, len(peers))
            for k in (1, 2, 3):
                go(fsend(k))
            ystart(2)
        else:
            ystart(0)
            ystart(1)
    go(act_copy)
    for s in range(2):
        for lb in (2, 0, 1):
            ystep(lb, s)
    far()
    for lb in (2, 0, 1):
        ystep(lb, 2)
    ystep(3, 0)
    for lb in (2, 0, 1):
        ystep(lb, 3)
        yfinal(lb)
    for c in loads[2:]:
        c.wait()
    ystep(3, 1)
    adam(2)
    ystep(3, 2)
    adam(0)
    adam(1)
    ystep(3, 3)
    adam(3)
    for i in (O_FIRST, O_SECOND):
        stores[i].start()
        drains.append(stores[i].wait)
    for stage in (owner_a, owner_b, owner_c):
        for h in range(2):
            stage(h)
    wx(0)
    for j in (1, 2, 3):
        go(z0send(j))
    y0start(0)
    wx(1)
    y1start()
    y1step(0)
    y0step(0, 0)
    for j in (1, 2, 3):
        y0start(j)
    y1step(1)
    for s in range(3):
        y0step(0, s + 1)
        for j in (1, 2, 3):
            y0step(j, s)
        if s < 2:
            y1step(s + 2)
    replicated()
    act_copy.wait_recv()
    project(1, ready1)
    project(0, ready0)
    for h in (1, 0):
        kcopy(h).wait_recv()
        keys[:, pl.ds(pl.multiple_of((2 * h + 1 - r) * LB, LB), LB)] = krec[h]
    k_store = pltpu.make_async_copy(keys, okeys_hbm, out_sem.at[5])
    k_store.start()
    for drain in drains:
        drain()
    for k in (1, 2):
        tsend(k).wait_send()
    gsend().wait_send()
    for k in (1, 2, 3):
        msend(k).wait_send()

    @pl.when(lax.rem(x, 2) == r)
    def _():
        for k in (1, 2, 3):
            wxsend(0, k).wait_send()

    k_store.wait()


def hand_over(*refs):
    sem = refs[18]
    loads = [
        pltpu.make_async_copy(refs[i], refs[12 + i], sem.at[0, i]) for i in range(6)
    ]
    stores = [
        pltpu.make_async_copy(refs[12 + i], refs[6 + i], sem.at[1, i]) for i in range(6)
    ]
    for c in loads:
        c.start()
    for c, o in zip(loads, stores):
        c.wait()
        o.start()
    for o in stores:
        o.wait()


def body(act, cot, w, m, v, ra, rm, ga, gm):
    dma = pltpu.SemaphoreType.DMA
    flat = lambda a: a.reshape(ROWS, KV)
    out = pl.pallas_call(
        kernel,
        out_shape=[jax.ShapeDtypeStruct((ROWS, KV), F32)] * 5
        + [jax.ShapeDtypeStruct((TOK, KV), BF)],
        in_specs=[pl.BlockSpec(memory_space=pl.ANY)] * 9,
        out_specs=[pl.BlockSpec(memory_space=pl.ANY)] * 6,
        scratch_shapes=[
            pltpu.VMEM((2, TOK, DW), BF),
            pltpu.VMEM((TOK, KV), BF),
            pltpu.VMEM((7, ROWS, KV), F32),
            pltpu.VMEM((4, N_Y, N_ZL, ROWS, LB), BF),
            pltpu.VMEM((2, 3, 4, N_ZL, ROWS, LB), BF),
            pltpu.VMEM((3, N_ZL, ROWS, LB), BF),
            pltpu.VMEM((3, N_ZL, ROWS, LB), BF),
            pltpu.VMEM((3, N_Y, ROWS, LB), BF),
            pltpu.VMEM((N_Y, ROWS, LB), BF),
            pltpu.VMEM((2, 4, ROWS, LB), BF),
            pltpu.VMEM((4, ROWS, LB), F32),
            pltpu.VMEM((N_X, ROWS, LB), F32),
            pltpu.VMEM((N_ZH, ROWS, LB), BF),
            pltpu.VMEM((2, ROWS, LB), F32),
            pltpu.VMEM((N_X, 2, ROWS, LB), F32),
            pltpu.VMEM((2, N_ZL, N_Y, ROWS, LB), BF),
            pltpu.VMEM((2, TOK, LB), BF),
            pltpu.VMEM((2, TOK, LB), BF),
            pltpu.VMEM((5, ROWS, KV), F32),
            pltpu.VMEM((TOK, KV), BF),
            dma((9,)),
            dma((6,)),
            dma((2,)),
            dma((2, 4, 4)),
            dma((2, 4, 4)),
            dma((3, 3)),
            dma((3, 3)),
            dma((3,)),
            dma((3,)),
            dma((4,)),
            dma((4,)),
            dma((2,)),
            dma((2,)),
            dma((2,)),
            dma((3,)),
            dma((4,)),
            dma((3,)),
            dma((2,)),
            dma((3,)),
            dma((3,)),
            dma((2, 4, 4)),
            dma((2, 4, 4)),
            dma((2, 4)),
            dma((2, 4)),
            dma((8, 3)),
            dma((8, 3)),
            dma((4,)),
        ],
        compiler_params=pltpu.CompilerParams(
            collective_id=0, has_side_effects=True, vmem_limit_bytes=60 * 1024 * 1024
        ),
        name="outer_sync",
    )(act, cot, *map(flat, (w, m, v, ra, rm, ga, gm)))
    first, second, rv, gv, gn, keys = pl.pallas_call(
        hand_over,
        out_shape=[jax.ShapeDtypeStruct(o.shape, o.dtype) for o in out],
        in_specs=[pl.BlockSpec(memory_space=pl.ANY)] * 6,
        out_specs=[pl.BlockSpec(memory_space=pl.ANY)] * 6,
        scratch_shapes=[pltpu.VMEM(o.shape, o.dtype) for o in out] + [dma((2, 6))],
        compiler_params=pltpu.CompilerParams(vmem_limit_bytes=60 * 1024 * 1024),
        name="hand_over",
    )(*out)
    return (
        first.reshape(1, 1, ROWS, KV),
        second.reshape(1, 1, ROWS, KV),
        rv.reshape(1, ROWS, KV),
        gv,
        gn,
        keys,
    )


def solution(mesh):
    finer = Mesh(
        mesh.devices.reshape(2, N_ZH, N_X, N_ZL, N_Y), ("region", "zh", "x", "zl", "y")
    )
    island = ("zh", "x")
    dev = ("zl", "y")
    every = ("region", "zh", "x", "zl", "y")
    return jax.shard_map(
        body,
        mesh=finer,
        in_specs=(
            P(every, None),
            P(every, None),
            P("region", island, dev, None),
            P("region", island, dev, None),
            P("region", island, dev, None),
            P("region", dev, None),
            P("region", dev, None),
            P(dev, None),
            P(dev, None),
        ),
        out_specs=(
            P("region", island, dev, None),
            P("region", island, dev, None),
            P("region", dev, None),
            P(dev, None),
            P(dev, None),
            P(every, None),
        ),
        check_vma=False,
    )
```
